32 devices in a mesh: fsdp: 4 (over y, core), expert: 8 (over z, x).
Axes of the slice: x: 2, y: 2, z: 4, core: 2. Of those that a mesh axis runs over, the one named last changes fastest.
Arguments:
- momentum: bfloat16 [16, 2, 2048, 768], P('expert', None, 'fsdp'), may hold values from -6 to 6
- gradient: bfloat16 [16, 2, 2048, 768], P('expert', None, 'fsdp'), may hold values from -70 to 70
- weights: bfloat16 [16, 2, 2048, 768], P('expert', None, 'fsdp'), may hold values from -0.03125 to 0.03125
- tokens: bfloat16 [2, 512, 2048], P(None, ('fsdp', 'expert')), may hold values from -24 to 24
- routes: int32 [2, 512, 8], P(None, ('fsdp', 'expert')), may hold values from 0 to 15, all different within a row; in each aligned block of 16 rows (0 to 15, 16 to 31, ..., all dimensions but the last counted through in order) at most 16 rows name the same one
- owners: int32 [4, 8], replicated, may hold values from 0 to 7, each once within a row
Outputs:
- hidden: bfloat16 [2, 4, 8, 32, 16, 384], P(None, 'fsdp', 'expert')
The draws below stay inside these ranges and needn't reach their ends.
Inputs may be any that keep to these rules, and one draw needn't show every extreme that they name: `routes`: in each batch, the 16 rows of one device name each expert at most 16 times, a bound that some block reaches; a row names 8 different experts. `owners`: each row is a permutation.
All inputs are finite; a program needn't handle non-finite values.
Results may differ from the reference program's by a relative error of at most 0.0095.
Values may be sent and summed in bfloat16 or wider, within the bound.
No kernel may reach another device: no remote copies, remote signals or barrier semaphores. Data moves between devices by JAX's collectives and lax.ppermute only.
A program may use at most 128 MiB of HBM per device.

```python
import math
import jax
import jax.numpy as jnp
import numpy as np
from jax import lax

D = 2048
FFE = 768
TOPK = 8
TOK_DEV = 16
EXP_DEV = 2
EXPERTS = 16
HALF = 384
SOURCES = 32
CAP = 16
TOKENS = 512
N_FSDP = 4
N_EXPERT = 8


def draw_gradient(key, part):

    def one_matrix(index):
        keys = jax.random.split(jax.random.fold_in(key, index), 4)
        noise = jnp.clip(jax.random.normal(keys[0], (D, FFE), jnp.float32), -5.0, 5.0)
        row_scale = jnp.exp(jax.random.uniform(keys[1], (D, 1), jnp.float32, 0.0, math.log(10.0)))
        column_scale = jnp.exp(jax.random.uniform(keys[2], (1, FFE), jnp.float32, 0.0, math.log(30.0)))
        mixing = jnp.clip(jax.random.normal(keys[3], (FFE, FFE), jnp.float32), -4.0, 4.0) / math.sqrt(FFE)
        scaled = noise * row_scale * column_scale
        mixed = jnp.dot(scaled, mixing, precision=lax.Precision.HIGHEST)
        return jnp.clip(0.05 * mixed, -70.0, 70.0)
    total = lax.map(one_matrix, jnp.arange(2 * EXPERTS, dtype=jnp.int32))
    return total.reshape(EXPERTS, 2, D, FFE).astype(jnp.bfloat16)


def block_levels(stream_key, dims, shards, least, largest):
    def one(position, parts):
        draws = jax.random.uniform(jax.random.fold_in(jax.random.fold_in(stream_key, 6), position), (parts,), jnp.float32, least / len(shards), largest / len(shards))
        return jnp.repeat(jnp.exp(draws), dims[position] // parts).reshape((-1,) + (1,) * (len(dims) - position - 1))

    level = one(*shards[0])
    for cut in shards[1:]:
        level = level * one(*cut)
    return level


def shared_out(key, own, number, rows, number_of, top, reach, lean):
    order = jax.random.permutation(key, number_of)
    heavy_load, usual = portions_of(number_of, rows * top, reach, lean, True), portions_of(number_of, rows * top, reach, lean, False)
    places = jnp.arange(number_of)

    def named(sizes, turn):
        used = int((sizes > 0).sum())
        fixed = max(1, used // 4)
        passed = fixed + (places - fixed + turn * (used - fixed)) % max(1, number_of - fixed)
        return jnp.zeros((number_of,), jnp.int32).at[order[jnp.where(places < fixed, places, passed)]].set(jnp.asarray(sizes, jnp.int32))

    sizes = jnp.where(number % 4 == 0, named(heavy_load, number // 4), named(usual, number - number // 4 - 1))
    mixed = jax.random.permutation(jax.random.fold_in(own, 3), number_of)
    donor, sink = mixed[0:number_of // 2 * 2:2], mixed[1:number_of // 2 * 2:2]
    margin = jnp.minimum(sizes[donor] - 1, reach - sizes[sink]) // 2
    margin = jnp.where((donor == order[0]) | (sink == order[0]) | (sizes[sink] == 0), 0, jnp.maximum(margin, 0))
    passed = jax.random.randint(jax.random.fold_in(own, 4), (number_of // 2,), 0, 1 << 20) % (margin + 1)
    sizes = sizes.at[donor].add(-passed).at[sink].add(passed)
    members = jnp.searchsorted(jnp.cumsum(sizes), jnp.arange(rows * top), side="right").astype(jnp.int32)
    listing = members.reshape(top, rows).T
    listing = listing[jax.random.permutation(jax.random.fold_in(own, 1), rows)]
    turn = jax.random.randint(jax.random.fold_in(own, 2), (rows, 1), 0, top)
    return jnp.take_along_axis(listing, (jnp.arange(top)[None, :] + turn) % top, axis=1)


def portions_of(number_of, total, limit, lean, full):
    loads = [(1 << 20) // math.isqrt(rank ** lean) + 1 for rank in range(1, number_of + 1)]
    largest = limit if full else min(limit, max(-(-total // number_of), total * loads[0] // sum(loads)))
    least = 1 if total - largest >= number_of - 1 else 0
    given, rest = [largest] + [least] * (number_of - 1), total - largest - least * (number_of - 1)
    while rest > 0:
        movable = [i for i in range(1, number_of) if given[i] < largest] or [i for i in range(1, number_of) if given[i] < limit]
        whole, remaining = sum([loads[i] for i in movable]), rest
        for i in movable:
            addition = min(limit - given[i], max(1, remaining * loads[i] // whole), rest)
            given[i] = given[i] + addition
            rest = rest - addition
    return np.array(given)


def gaussian(rng, dims, deviation, limit, cuts=(), kind=jnp.bfloat16):
    loudness = block_levels(rng, dims, cuts, -0.22, 0.18) if cuts else 1.0
    values = jax.random.normal(rng, dims, jnp.float32) * deviation * loudness
    return jnp.minimum(jnp.maximum(values, -limit), limit).astype(kind)


def setup_inputs(seed: int = 0) -> dict:
    key_of = jax.random.split(jax.random.key(seed), 7)
    momentum = gaussian(key_of[0], (EXPERTS, 2, D, FFE), 1.0, 6.0, ((0, 8), (2, 4)))
    gradient = draw_gradient(jax.random.fold_in(key_of[6], 71), 0)
    weights = gaussian(key_of[2], (EXPERTS, 2, D, FFE), (16 * D) ** -0.5, 0.03125, ((0, 8), (2, 4)))
    tokens = gaussian(key_of[3], (2, TOKENS, D), 4.0, 24.0, ((1, 32),))
    routes_keys = jax.random.split(jax.random.fold_in(key_of[4], 1), 2 * TOKENS // TOK_DEV)
    routes_turns = jax.random.permutation(jax.random.fold_in(key_of[4], 3), 2 * TOKENS // TOK_DEV)
    routes = jax.vmap(lambda own, number: shared_out(jax.random.fold_in(key_of[4], 2), own, number, TOK_DEV, EXPERTS, TOPK, CAP, 2))(routes_keys, routes_turns).reshape((2, TOKENS, TOPK))
    owners = jax.vmap(lambda own: jax.random.permutation(own, N_EXPERT))(jax.random.split(key_of[5], N_FSDP)).reshape((N_FSDP, N_EXPERT)).astype(jnp.int32)
    return dict(momentum=momentum, gradient=gradient, weights=weights, tokens=tokens, routes=routes, owners=owners)


momentum_decay = 0.95
coef_first = 3.4445
coef_second = -4.775
coef_third = 2.0315
step_size = 0.02
eps = 1e-07

def orthogonalize(update):
    values = update.astype(jnp.float32)
    squares_total = jnp.sum(values * values)
    current = (values / (jnp.sqrt(squares_total) + eps)).astype(jnp.bfloat16)
    for iteration in range(2):
        gram_matrix = lax.dot_general(current, current, (((0,), (0,)), ((), ())), preferred_element_type=jnp.float32).astype(jnp.bfloat16)
        square = jnp.dot(gram_matrix, gram_matrix, preferred_element_type=jnp.float32)
        polynomial = (coef_second * gram_matrix.astype(jnp.float32) + coef_third * square).astype(jnp.bfloat16)
        current = (coef_first * current.astype(jnp.float32) + jnp.dot(current, polynomial, preferred_element_type=jnp.float32)).astype(jnp.bfloat16)
    return current

def listed_rows(block_rows, block_routes):
    labels = jnp.arange(EXPERTS, dtype=jnp.int32)
    routed = jnp.any(block_routes[:, :, None] == labels[None, None, :], axis=1).astype(jnp.int32)
    before = jnp.cumsum(routed, axis=0) - routed
    slot_ids = jnp.arange(CAP, dtype=jnp.int32)
    select = ((routed[None, :, :] == 1) & (before[None, :, :] == slot_ids[:, None, None])).astype(jnp.float32)
    listed = jnp.einsum('qtx,td->xqd', select, block_rows.astype(jnp.float32))
    return listed.astype(jnp.bfloat16)

def reference(momentum, gradient, weights, tokens, routes, owners):
    update_scale = step_size * 0.2 * math.sqrt(max(D, FFE))

    def new_matrix(operands):
        moment, grad_part, weight_part = operands
        accumulated = momentum_decay * moment.astype(jnp.float32) + grad_part.astype(jnp.float32)
        update = (grad_part.astype(jnp.float32) + momentum_decay * accumulated).astype(jnp.bfloat16)
        orthogonal = orthogonalize(update)
        return (weight_part.astype(jnp.float32) - update_scale * orthogonal.astype(jnp.float32)).astype(jnp.bfloat16)
    renewed = lax.map(new_matrix, (momentum.reshape(-1, D, FFE), gradient.reshape(-1, D, FFE), weights.reshape(-1, D, FFE)))
    renewed = renewed.reshape(EXPERTS, 2, D, FFE)

    def block_lists(operands):
        block_rows, block_routes = operands
        return listed_rows(block_rows, block_routes)
    listed = lax.map(block_lists, (tokens.reshape(2 * SOURCES, TOK_DEV, D), routes.reshape(2 * SOURCES, TOK_DEV, TOPK)))
    listed = listed.reshape(2, SOURCES, EXPERTS, CAP, D)

    def owner_rows(owner_index):
        owner_row = owner_index // N_EXPERT
        owner_column = owner_index % N_EXPERT
        source_group = owners[owner_row, owner_column]
        expert = (source_group * EXP_DEV + owner_row // 2).astype(jnp.int32)
        half_index = (owner_row % 2).astype(jnp.int32)
        pair_weights = lax.dynamic_index_in_dim(renewed, expert, 0, keepdims=False)
        gate_half = lax.dynamic_slice_in_dim(pair_weights[0], half_index * HALF, HALF, 1)
        up_half = lax.dynamic_slice_in_dim(pair_weights[1], half_index * HALF, HALF, 1)
        combined = jnp.concatenate([gate_half, up_half], axis=1)
        gathered_rows = lax.dynamic_index_in_dim(listed, expert, 2, keepdims=False)
        product = jnp.dot(gathered_rows.reshape(-1, D), combined, preferred_element_type=jnp.float32)
        result = jax.nn.silu(product[:, :HALF]) * product[:, HALF:]
        return result.astype(jnp.bfloat16).reshape(2, SOURCES, CAP, HALF)
    hidden = lax.map(owner_rows, jnp.arange(N_FSDP * N_EXPERT, dtype=jnp.int32))
    hidden = hidden.reshape(N_FSDP, N_EXPERT, 2, SOURCES, CAP, HALF).transpose(2, 0, 1, 3, 4, 5)
    return hidden
```

```python
import functools
import math

import jax
import jax.numpy as jnp
import numpy as np
from jax import lax
from jax.experimental import pallas as pl
from jax.experimental.pallas import tpu as pltpu
from jax.sharding import PartitionSpec as P


momentum_decay = 0.95
coef_first = 3.4445
coef_second = -4.775
coef_third = 2.0315
step_size = 0.02
eps = 1e-07


VMEM = pl.BlockSpec(memory_space=pltpu.VMEM)
SMEM = pl.BlockSpec(memory_space=pltpu.SMEM)


def dot(a, b):
    return jnp.dot(a, b, preferred_element_type=jnp.float32)


def swapped(shard, axis, mask):
    return lax.ppermute(shard, axis, [(i, i ^ mask) for i in range(lax.axis_size(axis))])


def moved_along(shard, shift):
    size = lax.axis_size("expert")
    pairs = [(i, i + 2 * shift) for i in range(size) if 0 <= i + 2 * shift < size]
    return lax.ppermute(shard, "expert", pairs)


def slots_of(routes, experts):
    labels = lax.broadcasted_iota(jnp.int32, (1, 1, 1, experts), 3)
    routed = jnp.any(routes[:, :, :, None] == labels, axis=2).astype(jnp.int32)
    count = routes.shape[1]
    later = lax.broadcasted_iota(jnp.int32, (count, count), 0)
    earlier = lax.broadcasted_iota(jnp.int32, (count, count), 1)
    upto = (earlier <= later).astype(jnp.int32)
    place = jnp.sum(upto[None, :, :, None] * routed[:, None, :, :], axis=2)
    return jnp.where(routed == 1, place, 0)


def gathered(block):
    fsdp_size, group_size = lax.axis_size("fsdp"), lax.axis_size("expert")
    f, r = lax.axis_index("fsdp"), lax.axis_index("expert")
    held, masks = block[None], [0]
    if group_size == 8:
        mask = 2
        while mask < fsdp_size:
            held = jnp.concatenate([held, swapped(held, "fsdp", mask)])
            masks += [m ^ mask for m in masks]
            mask *= 2
        up, down = moved_along(held, 1), moved_along(held, -1)
        up2, down2 = moved_along(up, 1), moved_along(down, -1)
        up3, down3 = moved_along(up2, 1), moved_along(down2, -1)
        first = swapped(held, "expert", 1)
        near = jnp.concatenate([up, down])
        near_x = swapped(near, "expert", 1)
        far = up2 + down2
        far_x = swapped(far, "expert", 1)
        ends = up3 + down3
        ends_x = swapped(ends, "expert", 1)
        rows = jnp.concatenate([held, near, far, ends, first, near_x, far_x, ends_x])
        z, x = r // 2, r % 2
        layers = jnp.stack([z, z - 1, z + 1, z ^ 2, z ^ 3])
        layers = jnp.clip(layers, 0, group_size // 2 - 1)
        across = jnp.concatenate([layers * 2 + x, layers * 2 + (x ^ 1)])
        source_r = jnp.repeat(across, len(masks))
        source_f = jnp.tile(f ^ np.array(masks, np.int32), 10)
        return rows, source_f // 2, source_r
    held = lax.all_gather(block, "expert")
    mask = 2
    while mask < fsdp_size:
        held = jnp.concatenate([held, swapped(held, "fsdp", mask)])
        masks += [m ^ mask for m in masks]
        mask *= 2
    source_f = jnp.repeat(f ^ np.array(masks, np.int32), group_size)
    source_r = jnp.tile(jnp.arange(group_size, dtype=jnp.int32), len(masks))
    return held, source_f // 2, source_r


def columns_of(index, width):
    return pl.ds(pl.multiple_of(index * width, 128), width)


def started(*pairs_and_sem):
    *pairs, sem = pairs_and_sem
    copies = [pltpu.make_async_copy(src, dst, sem.at[i]) for i, (src, dst) in enumerate(pairs)]
    for copy in copies:
        copy.start()
    return copies


def factor_kernel(*refs):
    count = len(refs) - 4
    update_refs, (factor_ref, inverse_ref, held, sem) = refs[:count], refs[count:]
    copies = started(*[(u, held.at[i]) for i, u in enumerate(update_refs)], sem)
    gram = None
    for i, copy in enumerate(copies):
        copy.wait()
        rows = held[i]
        term = lax.dot_general(
            rows, rows, (((0,), (0,)), ((), ())), preferred_element_type=jnp.float32
        )
        gram = term if gram is None else gram + term
    diagonal = lax.broadcasted_iota(jnp.int32, gram.shape, 0) == lax.broadcasted_iota(
        jnp.int32, gram.shape, 1
    )
    inverse = 1.0 / (jnp.sqrt(jnp.sum(jnp.where(diagonal, gram, 0.0))) + eps)
    inverse_ref[0] = inverse
    gram0 = gram * inverse * inverse
    g0 = gram0.astype(jnp.bfloat16)
    p0 = (coef_second * gram0 + coef_third * dot(g0, g0)).astype(jnp.bfloat16)
    half_way = coef_first * gram0 + dot(g0, p0)
    gram1 = coef_first * half_way + dot(half_way.astype(jnp.bfloat16), p0)
    g1 = gram1.astype(jnp.bfloat16)
    p1 = (coef_second * gram1 + coef_third * dot(g1, g1)).astype(jnp.bfloat16)
    factor = coef_first * (p0.astype(jnp.float32) + p1.astype(jnp.float32)) + dot(p0, p1)
    factor_ref[...] = factor.astype(jnp.bfloat16)


def row_copies(order, at_ref, own_ref, other_ref, held):
    pairs = []
    for i, place in enumerate(order):
        columns = columns_of(at_ref[0] ^ place, held.shape[3])
        pairs.append((own_ref.at[:, columns], held.at[0, i]))
        pairs.append((other_ref.at[:, columns], held.at[1, i]))
    return pairs


def moved_kernel(order, at_ref, inverse_ref, factor_ref, own_ref, other_ref, *refs):
    count = len(order)
    update_refs = refs[:count]
    kept_ref, sent_ref, rows, update, factor, total, sem_u, sem_r, sem_f = refs[count:]
    pairs = row_copies(order, at_ref, own_ref, other_ref, rows)
    first = started(*[(u, update.at[i]) for i, u in enumerate(update_refs)], sem_u)
    second = started(*pairs, sem_r)
    (last,) = started((factor_ref, factor), sem_f)
    for i in range(count):
        first[i].wait()
        for side in range(2):
            second[2 * i + side].wait()
            term = dot(rows[side, i], update[i])
            total[side] = term if i == 0 else total[side] + term
    last.wait()
    width = kept_ref.shape[2]
    kind = lax.rem(at_ref[0], 2)
    for side in range(2):
        along = total[side] * inverse_ref[0]
        moved = coef_first * coef_first * along + dot(along.astype(jnp.bfloat16), factor[...])
        moved = moved.astype(jnp.bfloat16)
        left, right = moved[:, :width], moved[:, width:]
        kept_ref[side] = jnp.where(kind == 0, left, right)
        sent_ref[1 - side] = jnp.where(kind == 0, right, left)


def base_kernel(order, scale, at_ref, own_ref, other_ref, kept_ref, partner_ref, *refs):
    count = len(order)
    weight_refs = refs[:count]
    base_ref, rows, weight, moved, sem_w, sem_r, sem_m = refs[count:]
    first = started(*[(w, weight.at[i]) for i, w in enumerate(weight_refs)], sem_w)
    second = started(*row_copies(order, at_ref, own_ref, other_ref, rows), sem_r)
    third = started((kept_ref, moved.at[0]), (partner_ref, moved.at[1]), sem_m)
    for copy in first + second + third:
        copy.wait()
    width = moved.shape[3]
    own_kind = lax.rem(at_ref[0], 2)
    for side in range(2):
        for kind in range(2):
            part = jnp.where(own_kind == kind, moved[0, side], moved[1, side])
            total = -scale * part.astype(jnp.float32)
            for i in range(count):
                total += dot(rows[side, i], weight[i, kind])
            base_ref[side, :, kind * width : (kind + 1) * width] = total


def finish_kernel(order, group_size, at_ref, own_ref, other_ref, base_ref, *refs):
    count = len(order)
    weight_refs, refs = refs[:count], refs[count:]
    out_refs, (rows, weight, base, hidden, sem_w, sem_r, sem_b) = refs[:group_size], refs[group_size:]
    third = started(*[(base_ref.at[side], base.at[side]) for side in range(2)], sem_b)
    second = started(*row_copies(order, at_ref, own_ref, other_ref, rows), sem_r)
    first = started(*[(w, weight.at[i]) for i, w in enumerate(weight_refs)], sem_w)
    for copy in first:
        copy.wait()
    width = base.shape[2] // 2
    for side in range(2):
        third[side].wait()
        for i in range(count):
            second[2 * i + side].wait()
        products = []
        for kind in range(2):
            total = base[side, :, kind * width : (kind + 1) * width]
            for i in range(count):
                total += dot(rows[side, i], weight[i, kind])
            products.append(total)
        gate, up = products
        hidden[side] = (gate / (1.0 + jnp.exp(-gate)) * up).astype(jnp.bfloat16)
    chunk = hidden.shape[1] // group_size
    for mask in range(group_size):
        start = pl.multiple_of((at_ref[1] ^ mask) * chunk, chunk)
        out_refs[mask][...] = hidden[:, pl.ds(start, chunk), :]


def on_device(momentum, gradient, weights, tokens, routes, owners):
    fsdp_size = lax.axis_size("fsdp")
    group_size = lax.axis_size("expert")
    per_group = fsdp_size // 2
    experts = per_group * group_size
    local_rows = momentum.shape[2]
    hidden_width = momentum.shape[3]
    half_width = hidden_width // 2
    model_width = tokens.shape[2]
    tok_dev = tokens.shape[1]
    top_count = routes.shape[2]
    capacity = max(2, 2 * tok_dev * top_count // experts)
    f = lax.axis_index("fsdp")
    r = lax.axis_index("expert")
    own_expert = r * per_group + f // 2
    at = jnp.stack([f, r]).astype(jnp.int32)
    near = [0, 1]
    far = list(range(2, fsdp_size))
    order = near + far

    slot_lanes = -(-experts // 128) * 128
    slots = slots_of(routes, experts).astype(jnp.bfloat16)
    slots = jnp.pad(slots, ((0, 0), (0, 0), (0, slot_lanes - experts)))
    block = jnp.concatenate([tokens, slots], axis=2).reshape(2 * tok_dev, model_width + slot_lanes)
    blocks, source_pair, source_group = gathered(block)
    all_rows = blocks.reshape(-1, model_width + slot_lanes)
    lane = lax.broadcasted_iota(jnp.int32, (1, slot_lanes), 1)
    picked = jnp.where(lane == own_expert, all_rows[:, model_width:].astype(jnp.float32), 0.0)
    slot = jnp.sum(picked, axis=1).astype(jnp.int32).reshape(-1, 2, tok_dev)
    batch = jnp.arange(2, dtype=jnp.int32)[None, :, None]
    first = (source_group[:, None, None] * 2 + batch) * per_group + source_pair[:, None, None]
    listed_at = jnp.where(slot > 0, first * capacity + slot - 1, -1).reshape(1, -1)
    half_rows = group_size * 2 * per_group * capacity
    labels = lax.broadcasted_iota(jnp.int32, (half_rows, listed_at.shape[1]), 0)
    select = (labels == listed_at).astype(jnp.bfloat16)
    own_rows = dot(select, all_rows[:, :model_width]).astype(jnp.bfloat16)
    other_rows = swapped(own_rows, "fsdp", 1)

    moment = momentum.reshape(fsdp_size, local_rows, hidden_width)
    grad = gradient.reshape(fsdp_size, local_rows, hidden_width)
    weight = weights.reshape(fsdp_size, local_rows, hidden_width)
    update, held_weight = [None] * fsdp_size, [None] * fsdp_size
    for places in (far, near):
        for mask in reversed(places):
            moment_part = lax.dynamic_index_in_dim(moment, f ^ mask, 0, keepdims=False)
            grad_part = lax.dynamic_index_in_dim(grad, f ^ mask, 0, keepdims=False)
            grad_part = grad_part.astype(jnp.float32)
            accumulated = momentum_decay * moment_part.astype(jnp.float32) + grad_part
            update[mask] = (grad_part + momentum_decay * accumulated).astype(jnp.bfloat16)
        if places is far:
            moment, grad, *parts = lax.optimization_barrier(
                (moment, grad, *[update[m] for m in far])
            )
            for mask, part in zip(far, parts):
                update[mask] = part
    for mask in reversed(range(1, fsdp_size)):
        update[mask] = swapped(update[mask], "fsdp", mask)
    for mask in reversed(range(fsdp_size)):
        target = f ^ mask
        part = lax.dynamic_slice(
            weight,
            (target // 2 * 2, 0, target % 2 * half_width),
            (2, local_rows, half_width),
        )
        held_weight[mask] = swapped(part, "fsdp", mask) if mask else part

    full_rows = fsdp_size * local_rows
    update_scale = step_size * 0.2 * math.sqrt(max(full_rows, hidden_width))
    depth = local_rows
    any_ref = pl.BlockSpec(memory_space=pl.ANY)
    dma = pltpu.SemaphoreType.DMA
    bf16_scratch = lambda *shape: pltpu.VMEM(shape, jnp.bfloat16)
    shaped = lambda kind, *shape: jax.ShapeDtypeStruct(shape, kind)
    flops = 2 * 2 * half_rows * full_rows * hidden_width
    cost = lambda work, moved_bytes: pl.CostEstimate(
        flops=work, bytes_accessed=moved_bytes, transcendentals=0
    )
    factor, inverse = pl.pallas_call(
        factor_kernel,
        out_shape=[
            shaped(jnp.bfloat16, hidden_width, hidden_width),
            shaped(jnp.float32, 1),
        ],
        in_specs=[any_ref] * fsdp_size,
        out_specs=[VMEM, SMEM],
        scratch_shapes=[bf16_scratch(fsdp_size, depth, hidden_width), dma((fsdp_size,))],
        cost_estimate=cost(3 * flops, 4 << 20),
        name="factor",
    )(*[update[m] for m in order])

    kind = f % 2
    half_shape = (2, half_rows, half_width)
    count = len(order)
    kept, sent = pl.pallas_call(
        functools.partial(moved_kernel, order),
        out_shape=[shaped(jnp.bfloat16, *half_shape)] * 2,
        in_specs=[SMEM, SMEM] + [any_ref] * (3 + count),
        out_specs=[VMEM, VMEM],
        scratch_shapes=[
            bf16_scratch(2, count, half_rows, depth),
            bf16_scratch(count, depth, hidden_width),
            bf16_scratch(hidden_width, hidden_width),
            pltpu.VMEM((2, half_rows, hidden_width), jnp.float32),
            dma((count,)),
            dma((2 * count,)),
            dma((1,)),
        ],
        cost_estimate=cost(2 * flops, 12 << 20),
        name="moved",
    )(at, inverse, factor, own_rows, other_rows, *[update[m] for m in order])
    partner = swapped(sent, "fsdp", 1)
    count = len(near)
    base = pl.pallas_call(
        functools.partial(base_kernel, near, update_scale),
        out_shape=shaped(jnp.float32, 2, half_rows, hidden_width),
        in_specs=[SMEM] + [any_ref] * (4 + count),
        out_specs=VMEM,
        scratch_shapes=[
            bf16_scratch(2, count, half_rows, depth),
            bf16_scratch(count, 2, depth, half_width),
            bf16_scratch(2, *half_shape),
            dma((count,)),
            dma((2 * count,)),
            dma((2,)),
        ],
        cost_estimate=cost(flops, 10 << 20),
        name="base",
    )(at, own_rows, other_rows, kept, partner, *[held_weight[m] for m in near])
    chunk = half_rows // group_size
    count = len(far)
    pieces = pl.pallas_call(
        functools.partial(finish_kernel, far, group_size),
        out_shape=[shaped(jnp.bfloat16, 2, chunk, half_width)] * group_size,
        in_specs=[SMEM] + [any_ref] * (3 + count),
        out_specs=[VMEM] * group_size,
        scratch_shapes=[
            bf16_scratch(2, count, half_rows, depth),
            bf16_scratch(count, 2, depth, half_width),
            pltpu.VMEM((2, half_rows, hidden_width), jnp.float32),
            bf16_scratch(*half_shape),
            dma((count,)),
            dma((2 * count,)),
            dma((2,)),
        ],
        cost_estimate=cost(flops, 10 << 20),
        name="finish",
    )(at, own_rows, other_rows, base, *[held_weight[m] for m in far])

    spread = [swapped(pieces[m], "expert", m) if m else pieces[m] for m in range(group_size)]
    spread = jnp.stack(spread)
    owner_row = lax.dynamic_index_in_dim(owners, f, 0, keepdims=False)
    hidden = jnp.zeros((2, per_group, 2, group_size, capacity, half_width), jnp.bfloat16)
    for mask in range(group_size):
        wanted = lax.dynamic_index_in_dim(owner_row, r ^ mask, 0, keepdims=False) ^ r
        part = lax.dynamic_index_in_dim(spread, wanted, 0, keepdims=False)
        part = swapped(part, "expert", mask) if mask else part
        part = part.reshape(2, 2, per_group, 1, 1, capacity, half_width)
        hidden = lax.dynamic_update_slice(hidden, part[0], (0, 0, kind, r ^ mask, 0, 0))
        hidden = lax.dynamic_update_slice(hidden, part[1], (0, 0, 1 - kind, r ^ mask, 0, 0))
    return hidden.reshape(2, 1, 1, fsdp_size * group_size, capacity, half_width)


def solution(mesh):
    in_specs = (
        P("expert", None, "fsdp", None),
        P("expert", None, "fsdp", None),
        P("expert", None, "fsdp", None),
        P(None, ("fsdp", "expert"), None),
        P(None, ("fsdp", "expert"), None),
        P(),
    )
    out_specs = P(None, "fsdp", "expert", None, None, None)

    return jax.shard_map(
        on_device, mesh=mesh, in_specs=in_specs, out_specs=out_specs, check_vma=False
    )
```

```python
import functools
import math

import jax
import jax.numpy as jnp
import numpy as np
from jax import lax
from jax.experimental import pallas as pl
from jax.experimental.pallas import tpu as pltpu
from jax.sharding import PartitionSpec as P


momentum_decay = 0.95
coef_first = 3.4445
coef_second = -4.775
coef_third = 2.0315
step_size = 0.02
eps = 1e-07


VMEM = pl.BlockSpec(memory_space=pltpu.VMEM)
SMEM = pl.BlockSpec(memory_space=pltpu.SMEM)


def dot(a, b):
    return jnp.dot(a, b, preferred_element_type=jnp.float32)


def swapped(shard, axis, mask):
    return lax.ppermute(shard, axis, [(i, i ^ mask) for i in range(lax.axis_size(axis))])


def slots_of(routes, experts):
    labels = lax.broadcasted_iota(jnp.int32, (1, 1, 1, experts), 3)
    routed = jnp.any(routes[:, :, :, None] == labels, axis=2).astype(jnp.int32)
    count = routes.shape[1]
    later = lax.broadcasted_iota(jnp.int32, (count, count), 0)
    earlier = lax.broadcasted_iota(jnp.int32, (count, count), 1)
    upto = (earlier <= later).astype(jnp.int32)
    place = jnp.sum(upto[None, :, :, None] * routed[:, None, :, :], axis=2)
    return jnp.where(routed == 1, place, 0)


def gathered(block):
    fsdp_size, group_size = lax.axis_size("fsdp"), lax.axis_size("expert")
    f, r = lax.axis_index("fsdp"), lax.axis_index("expert")
    held, masks = block[None], [0]
    if group_size == 8:
        mask = 2
        while mask < fsdp_size:
            held = jnp.concatenate([held, swapped(held, "fsdp", mask)])
            masks += [m ^ mask for m in masks]
            mask *= 2
        beside = swapped(held, "expert", 2)
        opposite = swapped(held, "expert", 6)
        across = [swapped(held, "expert", 1), swapped(beside, "expert", 1)]
        last = swapped(opposite, "expert", 2)
        across += [swapped(opposite, "expert", 1), swapped(last, "expert", 1)]
        rows = jnp.concatenate([held, beside, opposite, last, *across])
        source_r = jnp.repeat(r ^ np.array([0, 2, 6, 4, 1, 3, 7, 5], np.int32), len(masks))
        source_f = jnp.tile(f ^ np.array(masks, np.int32), 8)
        return rows, source_f // 2, source_r
    held = lax.all_gather(block, "expert")
    mask = 2
    while mask < fsdp_size:
        held = jnp.concatenate([held, swapped(held, "fsdp", mask)])
        masks += [m ^ mask for m in masks]
        mask *= 2
    source_f = jnp.repeat(f ^ np.array(masks, np.int32), group_size)
    source_r = jnp.tile(jnp.arange(group_size, dtype=jnp.int32), len(masks))
    return held, source_f // 2, source_r


def columns_of(index, width):
    return pl.ds(pl.multiple_of(index * width, 128), width)


def gram_of(update_refs, total):
    for rows_ref in update_refs:
        rows = rows_ref[...]
        term = lax.dot_general(
            rows, rows, (((0,), (0,)), ((), ())), preferred_element_type=jnp.float32
        )
        total = term if total is None else total + term
    return total


def gram_kernel(*refs):
    refs[-1][...] = gram_of(refs[:-1], None)


def factor_kernel(gram_ref, *refs):
    update_refs, (factor_ref, inverse_ref) = refs[:-2], refs[-2:]
    gram = gram_of(update_refs, gram_ref[...])
    diagonal = lax.broadcasted_iota(jnp.int32, gram.shape, 0) == lax.broadcasted_iota(
        jnp.int32, gram.shape, 1
    )
    inverse = 1.0 / (jnp.sqrt(jnp.sum(jnp.where(diagonal, gram, 0.0))) + eps)
    inverse_ref[0] = inverse
    gram0 = gram * inverse * inverse
    g0 = gram0.astype(jnp.bfloat16)
    p0 = (coef_second * gram0 + coef_third * dot(g0, g0)).astype(jnp.bfloat16)
    half_way = coef_first * gram0 + dot(g0, p0)
    gram1 = coef_first * half_way + dot(half_way.astype(jnp.bfloat16), p0)
    g1 = gram1.astype(jnp.bfloat16)
    p1 = (coef_second * gram1 + coef_third * dot(g1, g1)).astype(jnp.bfloat16)
    factor = coef_first * (p0.astype(jnp.float32) + p1.astype(jnp.float32)) + dot(p0, p1)
    factor_ref[...] = factor.astype(jnp.bfloat16)


def rows_at(at_ref, place, rows_ref, depth):
    return rows_ref[:, columns_of(at_ref[0] ^ place, depth)]


def along_kernel(order, scale, at_ref, inverse_ref, factor_ref, own_ref, other_ref, *refs):
    count = len(order)
    update_refs, weight_refs, (base_ref, sent_ref) = refs[:count], refs[count:-2], refs[-2:]
    width = sent_ref.shape[2]
    depth = update_refs[0].shape[0]
    own_kind = lax.rem(at_ref[0], 2)
    for side, rows_ref in enumerate((own_ref, other_ref)):
        total = sum(
            dot(rows_at(at_ref, place, rows_ref, depth), u[...])
            for place, u in zip(order, update_refs)
        )
        along = total * inverse_ref[0]
        moved = coef_first * coef_first * along + dot(along.astype(jnp.bfloat16), factor_ref[...])
        left, right = moved[:, :width], moved[:, width:]
        sent_ref[1 - side] = jnp.where(own_kind == 0, right, left).astype(jnp.bfloat16)
        kept = scale * jnp.where(own_kind == 0, left, right)
        for kind in range(2):
            product = sum(
                dot(rows_at(at_ref, place, rows_ref, depth), weight[kind])
                for place, weight in zip(order, weight_refs)
            )
            base_ref[kind, side] = product - jnp.where(own_kind == kind, kept, 0.0)


def finish_kernel(order, group_size, scale, at_ref, own_ref, other_ref, base_ref, moved_ref, *refs):
    count = len(order)
    weight_refs, out_refs, hidden = refs[:count], refs[count:-1], refs[-1]
    depth = weight_refs[0].shape[1]
    own_kind = lax.rem(at_ref[0], 2)
    for side, rows_ref in enumerate((own_ref, other_ref)):
        moved = scale * moved_ref[side].astype(jnp.float32)
        products = []
        for kind in range(2):
            total = base_ref[kind, side] - jnp.where(own_kind == kind, 0.0, moved)
            for place, weight in zip(order, weight_refs):
                total += dot(rows_at(at_ref, place, rows_ref, depth), weight[kind])
            products.append(total)
        gate, up = products
        hidden[side] = (gate / (1.0 + jnp.exp(-gate)) * up).astype(jnp.bfloat16)
    chunk = hidden.shape[1] // group_size
    for mask in range(group_size):
        start = pl.multiple_of((at_ref[1] ^ mask) * chunk, chunk)
        out_refs[mask][...] = hidden[:, pl.ds(start, chunk), :]


def choose_kernel(at_ref, owners_ref, *refs):
    held = refs[-1]
    count = held.shape[0]
    for mask in range(count):
        held[mask] = refs[mask][...]
    for mask in range(count):
        owner = owners_ref[at_ref[0], at_ref[1] ^ mask]
        refs[count + mask][...] = held[owner ^ at_ref[1]]


def on_device(momentum, gradient, weights, tokens, routes, owners):
    fsdp_size = lax.axis_size("fsdp")
    group_size = lax.axis_size("expert")
    per_group = fsdp_size // 2
    experts = per_group * group_size
    local_rows = momentum.shape[2]
    hidden_width = momentum.shape[3]
    half_width = hidden_width // 2
    model_width = tokens.shape[2]
    tok_dev = tokens.shape[1]
    top_count = routes.shape[2]
    capacity = max(2, 2 * tok_dev * top_count // experts)
    f = lax.axis_index("fsdp")
    r = lax.axis_index("expert")
    own_expert = r * per_group + f // 2
    at = jnp.stack([f, r]).astype(jnp.int32)
    near = [0, 1]
    far = list(range(2, fsdp_size))
    order = near + far

    slot_lanes = -(-experts // 128) * 128
    slots = slots_of(routes, experts).astype(jnp.bfloat16)
    slots = jnp.pad(slots, ((0, 0), (0, 0), (0, slot_lanes - experts)))
    block = jnp.concatenate([tokens, slots], axis=2).reshape(2 * tok_dev, model_width + slot_lanes)
    blocks, source_pair, source_group = gathered(block)
    all_rows = blocks.reshape(-1, model_width + slot_lanes)
    lane = lax.broadcasted_iota(jnp.int32, (1, slot_lanes), 1)
    picked = jnp.where(lane == own_expert, all_rows[:, model_width:].astype(jnp.float32), 0.0)
    slot = jnp.sum(picked, axis=1).astype(jnp.int32).reshape(-1, 2, tok_dev)
    batch = jnp.arange(2, dtype=jnp.int32)[None, :, None]
    first = (source_group[:, None, None] * 2 + batch) * per_group + source_pair[:, None, None]
    listed_at = jnp.where(slot > 0, first * capacity + slot - 1, -1).reshape(1, -1)
    half_rows = group_size * 2 * per_group * capacity
    labels = lax.broadcasted_iota(jnp.int32, (half_rows, listed_at.shape[1]), 0)
    select = (labels == listed_at).astype(jnp.bfloat16)
    own_rows = dot(select, all_rows[:, :model_width]).astype(jnp.bfloat16)
    other_rows = swapped(own_rows, "fsdp", 1)

    moment = momentum.reshape(fsdp_size, local_rows, hidden_width)
    grad = gradient.reshape(fsdp_size, local_rows, hidden_width)
    weight = weights.reshape(fsdp_size, local_rows, hidden_width)
    update, held_weight = [None] * fsdp_size, [None] * fsdp_size
    for places in (far, near):
        for mask in reversed(places):
            moment_part = lax.dynamic_index_in_dim(moment, f ^ mask, 0, keepdims=False)
            grad_part = lax.dynamic_index_in_dim(grad, f ^ mask, 0, keepdims=False)
            grad_part = grad_part.astype(jnp.float32)
            accumulated = momentum_decay * moment_part.astype(jnp.float32) + grad_part
            update[mask] = (grad_part + momentum_decay * accumulated).astype(jnp.bfloat16)
        if places is far:
            moment, grad, *parts = lax.optimization_barrier(
                (moment, grad, *[update[m] for m in far])
            )
            for mask, part in zip(far, parts):
                update[mask] = part
    for mask in reversed(range(1, fsdp_size)):
        update[mask] = swapped(update[mask], "fsdp", mask)
    for mask in reversed(range(fsdp_size)):
        target = f ^ mask
        part = lax.dynamic_slice(
            weight,
            (target // 2 * 2, 0, target % 2 * half_width),
            (2, local_rows, half_width),
        )
        held_weight[mask] = swapped(part, "fsdp", mask) if mask else part

    full_rows = fsdp_size * local_rows
    update_scale = step_size * 0.2 * math.sqrt(max(full_rows, hidden_width))
    bf16_scratch = lambda *shape: pltpu.VMEM(shape, jnp.bfloat16)
    shaped = lambda kind, *shape: jax.ShapeDtypeStruct(shape, kind)
    flops = 2 * 2 * half_rows * full_rows * hidden_width
    cost = lambda work, moved_bytes: pl.CostEstimate(
        flops=work, bytes_accessed=moved_bytes, transcendentals=0
    )
    limit = lambda mebibytes: pltpu.CompilerParams(vmem_limit_bytes=mebibytes << 20)
    early, late = near + far[1:], far[:1]
    gram = pl.pallas_call(
        gram_kernel,
        out_shape=shaped(jnp.float32, hidden_width, hidden_width),
        in_specs=[VMEM] * len(early),
        out_specs=VMEM,
        compiler_params=limit(8),
        cost_estimate=cost(flops, 4 << 20),
        name="gram",
    )(*[update[m] for m in early])
    factor, inverse = pl.pallas_call(
        factor_kernel,
        out_shape=[
            shaped(jnp.bfloat16, hidden_width, hidden_width),
            shaped(jnp.float32, 1),
        ],
        in_specs=[VMEM] * (1 + len(late)),
        out_specs=[VMEM, SMEM],
        compiler_params=limit(14),
        cost_estimate=cost(2 * flops, 4 << 20),
        name="factor",
    )(gram, *[update[m] for m in late])

    kind = f % 2
    half_shape = (2, half_rows, half_width)
    base, sent = pl.pallas_call(
        functools.partial(along_kernel, order, update_scale),
        out_shape=[
            shaped(jnp.float32, 2, *half_shape),
            shaped(jnp.bfloat16, *half_shape),
        ],
        in_specs=[SMEM, SMEM] + [VMEM] * (3 + len(order) + len(near)),
        out_specs=[VMEM, VMEM],
        cost_estimate=cost(2 * flops, 12 << 20),
        compiler_params=limit(10),
        name="along",
    )(
        at,
        inverse,
        factor,
        own_rows,
        other_rows,
        *[update[m] for m in order],
        *[held_weight[m] for m in near],
    )
    partner = swapped(sent, "fsdp", 1)
    chunk = half_rows // group_size
    pieces = pl.pallas_call(
        functools.partial(finish_kernel, far, group_size, update_scale),
        out_shape=[shaped(jnp.bfloat16, 2, chunk, half_width)] * group_size,
        in_specs=[SMEM] + [VMEM] * (4 + len(far)),
        out_specs=[VMEM] * group_size,
        scratch_shapes=[bf16_scratch(*half_shape)],
        cost_estimate=cost(flops, 10 << 20),
        compiler_params=limit(8),
        name="finish",
    )(at, own_rows, other_rows, base, partner, *[held_weight[m] for m in far])

    spread = [swapped(pieces[m], "expert", m) if m else pieces[m] for m in range(group_size)]
    part_shape = spread[0].shape
    chosen = pl.pallas_call(
        choose_kernel,
        out_shape=[shaped(jnp.bfloat16, *part_shape)] * group_size,
        in_specs=[SMEM, SMEM] + [VMEM] * group_size,
        out_specs=[VMEM] * group_size,
        scratch_shapes=[bf16_scratch(group_size, *part_shape)],
        cost_estimate=cost(0, 2 << 20),
        compiler_params=limit(8),
        name="choose",
    )(at, owners, *spread)
    hidden = jnp.zeros((2, per_group, 2, group_size, capacity, half_width), jnp.bfloat16)
    for mask in range(group_size):
        part = chosen[mask]
        part = swapped(part, "expert", mask) if mask else part
        part = part.reshape(2, 2, per_group, 1, 1, capacity, half_width)
        hidden = lax.dynamic_update_slice(hidden, part[0], (0, 0, kind, r ^ mask, 0, 0))
        hidden = lax.dynamic_update_slice(hidden, part[1], (0, 0, 1 - kind, r ^ mask, 0, 0))
    return hidden.reshape(2, 1, 1, fsdp_size * group_size, capacity, half_width)


def solution(mesh):
    in_specs = (
        P("expert", None, "fsdp", None),
        P("expert", None, "fsdp", None),
        P("expert", None, "fsdp", None),
        P(None, ("fsdp", "expert"), None),
        P(None, ("fsdp", "expert"), None),
        P(),
    )
    out_specs = P(None, "fsdp", "expert", None, None, None)

    return jax.shard_map(
        on_device, mesh=mesh, in_specs=in_specs, out_specs=out_specs, check_vma=False
    )
```

```python
import functools
import math

import jax
import jax.numpy as jnp
import numpy as np
from jax import lax
from jax.experimental import pallas as pl
from jax.experimental.pallas import tpu as pltpu
from jax.sharding import PartitionSpec as P


momentum_decay = 0.95
coef_first = 3.4445
coef_second = -4.775
coef_third = 2.0315
step_size = 0.02
eps = 1e-07


VMEM = pl.BlockSpec(memory_space=pltpu.VMEM)
SMEM = pl.BlockSpec(memory_space=pltpu.SMEM)


def dot(a, b):
    return jnp.dot(a, b, preferred_element_type=jnp.float32)


def swapped(shard, axis, mask):
    return lax.ppermute(shard, axis, [(i, i ^ mask) for i in range(lax.axis_size(axis))])


def slots_of(routes, experts):
    labels = lax.broadcasted_iota(jnp.int32, (1, 1, 1, experts), 3)
    routed = jnp.any(routes[:, :, :, None] == labels, axis=2).astype(jnp.int32)
    count = routes.shape[1]
    later = lax.broadcasted_iota(jnp.int32, (count, count), 0)
    earlier = lax.broadcasted_iota(jnp.int32, (count, count), 1)
    upto = (earlier <= later).astype(jnp.int32)
    place = jnp.sum(upto[None, :, :, None] * routed[:, None, :, :], axis=2)
    return jnp.where(routed == 1, place, 0)


def gathered(block):
    fsdp_size, group_size = lax.axis_size("fsdp"), lax.axis_size("expert")
    f, r = lax.axis_index("fsdp"), lax.axis_index("expert")
    held, masks = block[None], [0]
    if group_size == 8:
        mask = 2
        while mask < fsdp_size:
            held = jnp.concatenate([held, swapped(held, "fsdp", mask)])
            masks += [m ^ mask for m in masks]
            mask *= 2
        beside = swapped(held, "expert", 2)
        opposite = swapped(held, "expert", 6)
        across = [swapped(held, "expert", 1), swapped(beside, "expert", 1)]
        last = swapped(opposite, "expert", 2)
        across += [swapped(opposite, "expert", 1), swapped(last, "expert", 1)]
        rows = jnp.concatenate([held, beside, opposite, last, *across])
        source_r = jnp.repeat(r ^ np.array([0, 2, 6, 4, 1, 3, 7, 5], np.int32), len(masks))
        source_f = jnp.tile(f ^ np.array(masks, np.int32), 8)
        return rows, source_f // 2, source_r
    held = lax.all_gather(block, "expert")
    mask = 2
    while mask < fsdp_size:
        held = jnp.concatenate([held, swapped(held, "fsdp", mask)])
        masks += [m ^ mask for m in masks]
        mask *= 2
    source_f = jnp.repeat(f ^ np.array(masks, np.int32), group_size)
    source_r = jnp.tile(jnp.arange(group_size, dtype=jnp.int32), len(masks))
    return held, source_f // 2, source_r


def columns_of(index, width):
    return pl.ds(pl.multiple_of(index * width, 128), width)


def gram_of(update_refs, total):
    for rows_ref in update_refs:
        rows = rows_ref[...]
        term = lax.dot_general(
            rows, rows, (((0,), (0,)), ((), ())), preferred_element_type=jnp.float32
        )
        total = term if total is None else total + term
    return total


def gram_kernel(*refs):
    refs[-1][...] = gram_of(refs[:-1], None)


def factor_kernel(gram_ref, *refs):
    update_refs, (factor_ref, inverse_ref) = refs[:-2], refs[-2:]
    gram = gram_of(update_refs, gram_ref[...])
    diagonal = lax.broadcasted_iota(jnp.int32, gram.shape, 0) == lax.broadcasted_iota(
        jnp.int32, gram.shape, 1
    )
    inverse = 1.0 / (jnp.sqrt(jnp.sum(jnp.where(diagonal, gram, 0.0))) + eps)
    inverse_ref[0] = inverse
    gram0 = gram * inverse * inverse
    g0 = gram0.astype(jnp.bfloat16)
    p0 = (coef_second * gram0 + coef_third * dot(g0, g0)).astype(jnp.bfloat16)
    half_way = coef_first * gram0 + dot(g0, p0)
    gram1 = coef_first * half_way + dot(half_way.astype(jnp.bfloat16), p0)
    g1 = gram1.astype(jnp.bfloat16)
    p1 = (coef_second * gram1 + coef_third * dot(g1, g1)).astype(jnp.bfloat16)
    factor = coef_first * (p0.astype(jnp.float32) + p1.astype(jnp.float32)) + dot(p0, p1)
    factor_ref[...] = factor.astype(jnp.bfloat16)


def rows_at(at_ref, place, rows_ref, depth):
    return rows_ref[:, columns_of(at_ref[0] ^ place, depth)]


def along_kernel(order, sooner, scale, at_ref, inverse_ref, factor_ref, own_ref, other_ref, *refs):
    count = len(order)
    update_refs, weight_refs, (base_ref, sent_ref) = refs[:count], refs[count:-2], refs[-2:]
    width = sent_ref.shape[2]
    depth = update_refs[0].shape[0]
    own_kind = lax.rem(at_ref[0], 2)
    for side, rows_ref in enumerate((own_ref, other_ref)):
        total = sum(
            dot(rows_at(at_ref, place, rows_ref, depth), u[...])
            for place, u in zip(order, update_refs)
        )
        along = total * inverse_ref[0]
        moved = coef_first * coef_first * along + dot(along.astype(jnp.bfloat16), factor_ref[...])
        left, right = moved[:, :width], moved[:, width:]
        sent_ref[1 - side] = jnp.where(own_kind == 0, right, left).astype(jnp.bfloat16)
        kept = scale * jnp.where(own_kind == 0, left, right)
        for kind in range(2):
            product = sum(
                dot(rows_at(at_ref, place, rows_ref, depth), weight[kind])
                for place, weight in zip(sooner, weight_refs)
            )
            base_ref[kind, side] = product - jnp.where(own_kind == kind, kept, 0.0)


def finish_kernel(order, group_size, scale, at_ref, own_ref, other_ref, base_ref, moved_ref, *refs):
    count = len(order)
    weight_refs, out_refs, hidden = refs[:count], refs[count:-1], refs[-1]
    depth = weight_refs[0].shape[1]
    own_kind = lax.rem(at_ref[0], 2)
    for side, rows_ref in enumerate((own_ref, other_ref)):
        moved = scale * moved_ref[side].astype(jnp.float32)
        products = []
        for kind in range(2):
            total = base_ref[kind, side] - jnp.where(own_kind == kind, 0.0, moved)
            for place, weight in zip(order, weight_refs):
                total += dot(rows_at(at_ref, place, rows_ref, depth), weight[kind])
            products.append(total)
        gate, up = products
        hidden[side] = (gate / (1.0 + jnp.exp(-gate)) * up).astype(jnp.bfloat16)
    chunk = hidden.shape[1] // group_size
    for mask in range(group_size):
        start = pl.multiple_of((at_ref[1] ^ mask) * chunk, chunk)
        out_refs[mask][...] = hidden[:, pl.ds(start, chunk), :]


def choose_kernel(at_ref, owners_ref, *refs):
    held = refs[-1]
    count = held.shape[0]
    for mask in range(count):
        held[mask] = refs[mask][...]
    for mask in range(count):
        owner = owners_ref[at_ref[0], at_ref[1] ^ mask]
        refs[count + mask][...] = held[owner ^ at_ref[1]]


def on_device(momentum, gradient, weights, tokens, routes, owners):
    fsdp_size = lax.axis_size("fsdp")
    group_size = lax.axis_size("expert")
    per_group = fsdp_size // 2
    experts = per_group * group_size
    local_rows = momentum.shape[2]
    hidden_width = momentum.shape[3]
    half_width = hidden_width // 2
    model_width = tokens.shape[2]
    tok_dev = tokens.shape[1]
    top_count = routes.shape[2]
    capacity = max(2, 2 * tok_dev * top_count // experts)
    f = lax.axis_index("fsdp")
    r = lax.axis_index("expert")
    own_expert = r * per_group + f // 2
    at = jnp.stack([f, r]).astype(jnp.int32)
    near = [0, 1]
    far = list(range(2, fsdp_size))
    order = near + far
    sooner, latest = near + far[:0:-1], far[:1]

    slot_lanes = -(-experts // 128) * 128
    slots = slots_of(routes, experts).astype(jnp.bfloat16)
    slots = jnp.pad(slots, ((0, 0), (0, 0), (0, slot_lanes - experts)))
    block = jnp.concatenate([tokens, slots], axis=2).reshape(2 * tok_dev, model_width + slot_lanes)
    blocks, source_pair, source_group = gathered(block)
    all_rows = blocks.reshape(-1, model_width + slot_lanes)
    lane = lax.broadcasted_iota(jnp.int32, (1, slot_lanes), 1)
    picked = jnp.where(lane == own_expert, all_rows[:, model_width:].astype(jnp.float32), 0.0)
    slot = jnp.sum(picked, axis=1).astype(jnp.int32).reshape(-1, 2, tok_dev)
    batch = jnp.arange(2, dtype=jnp.int32)[None, :, None]
    first = (source_group[:, None, None] * 2 + batch) * per_group + source_pair[:, None, None]
    listed_at = jnp.where(slot > 0, first * capacity + slot - 1, -1).reshape(1, -1)
    half_rows = group_size * 2 * per_group * capacity
    labels = lax.broadcasted_iota(jnp.int32, (half_rows, listed_at.shape[1]), 0)
    select = (labels == listed_at).astype(jnp.bfloat16)
    own_rows = dot(select, all_rows[:, :model_width]).astype(jnp.bfloat16)
    other_rows = swapped(own_rows, "fsdp", 1)

    moment = momentum.reshape(fsdp_size, local_rows, hidden_width)
    grad = gradient.reshape(fsdp_size, local_rows, hidden_width)
    weight = weights.reshape(fsdp_size, local_rows, hidden_width)
    update, held_weight = [None] * fsdp_size, [None] * fsdp_size
    for places in (far, near):
        for mask in reversed(places):
            moment_part = lax.dynamic_index_in_dim(moment, f ^ mask, 0, keepdims=False)
            grad_part = lax.dynamic_index_in_dim(grad, f ^ mask, 0, keepdims=False)
            grad_part = grad_part.astype(jnp.float32)
            accumulated = momentum_decay * moment_part.astype(jnp.float32) + grad_part
            update[mask] = (grad_part + momentum_decay * accumulated).astype(jnp.bfloat16)
        if places is far:
            moment, grad, *parts = lax.optimization_barrier(
                (moment, grad, *[update[m] for m in far])
            )
            for mask, part in zip(far, parts):
                update[mask] = part
    for mask in reversed(range(1, fsdp_size)):
        update[mask] = swapped(update[mask], "fsdp", mask)
    for mask in reversed(range(fsdp_size)):
        target = f ^ mask
        part = lax.dynamic_slice(
            weight,
            (target // 2 * 2, 0, target % 2 * half_width),
            (2, local_rows, half_width),
        )
        held_weight[mask] = swapped(part, "fsdp", mask) if mask else part

    full_rows = fsdp_size * local_rows
    update_scale = step_size * 0.2 * math.sqrt(max(full_rows, hidden_width))
    bf16_scratch = lambda *shape: pltpu.VMEM(shape, jnp.bfloat16)
    shaped = lambda kind, *shape: jax.ShapeDtypeStruct(shape, kind)
    flops = 2 * 2 * half_rows * full_rows * hidden_width
    cost = lambda work, moved_bytes: pl.CostEstimate(
        flops=work, bytes_accessed=moved_bytes, transcendentals=0
    )
    limit = lambda mebibytes: pltpu.CompilerParams(vmem_limit_bytes=mebibytes << 20)
    early, late = near + far[1:], far[:1]
    gram = pl.pallas_call(
        gram_kernel,
        out_shape=shaped(jnp.float32, hidden_width, hidden_width),
        in_specs=[VMEM] * len(early),
        out_specs=VMEM,
        compiler_params=limit(8),
        cost_estimate=cost(flops, 4 << 20),
        name="gram",
    )(*[update[m] for m in early])
    factor, inverse = pl.pallas_call(
        factor_kernel,
        out_shape=[
            shaped(jnp.bfloat16, hidden_width, hidden_width),
            shaped(jnp.float32, 1),
        ],
        in_specs=[VMEM] * (1 + len(late)),
        out_specs=[VMEM, SMEM],
        compiler_params=limit(14),
        cost_estimate=cost(2 * flops, 4 << 20),
        name="factor",
    )(gram, *[update[m] for m in late])

    kind = f % 2
    half_shape = (2, half_rows, half_width)
    base, sent = pl.pallas_call(
        functools.partial(along_kernel, order, sooner, update_scale),
        out_shape=[
            shaped(jnp.float32, 2, *half_shape),
            shaped(jnp.bfloat16, *half_shape),
        ],
        in_specs=[SMEM, SMEM] + [VMEM] * (3 + len(order) + len(sooner)),
        out_specs=[VMEM, VMEM],
        cost_estimate=cost(2 * flops, 12 << 20),
        compiler_params=limit(10),
        name="along",
    )(
        at,
        inverse,
        factor,
        own_rows,
        other_rows,
        *[update[m] for m in order],
        *[held_weight[m] for m in sooner],
    )
    partner = swapped(sent, "fsdp", 1)
    chunk = half_rows // group_size
    pieces = pl.pallas_call(
        functools.partial(finish_kernel, latest, group_size, update_scale),
        out_shape=[shaped(jnp.bfloat16, 2, chunk, half_width)] * group_size,
        in_specs=[SMEM] + [VMEM] * (4 + len(latest)),
        out_specs=[VMEM] * group_size,
        scratch_shapes=[bf16_scratch(*half_shape)],
        cost_estimate=cost(flops, 10 << 20),
        compiler_params=limit(8),
        name="finish",
    )(at, own_rows, other_rows, base, partner, *[held_weight[m] for m in latest])

    spread = [swapped(pieces[m], "expert", m) if m else pieces[m] for m in range(group_size)]
    part_shape = spread[0].shape
    chosen = pl.pallas_call(
        choose_kernel,
        out_shape=[shaped(jnp.bfloat16, *part_shape)] * group_size,
        in_specs=[SMEM, SMEM] + [VMEM] * group_size,
        out_specs=[VMEM] * group_size,
        scratch_shapes=[bf16_scratch(group_size, *part_shape)],
        cost_estimate=cost(0, 2 << 20),
        compiler_params=limit(8),
        name="choose",
    )(at, owners, *spread)
    hidden = jnp.zeros((2, per_group, 2, group_size, capacity, half_width), jnp.bfloat16)
    for mask in range(group_size):
        part = chosen[mask]
        part = swapped(part, "expert", mask) if mask else part
        part = part.reshape(2, 2, per_group, 1, 1, capacity, half_width)
        hidden = lax.dynamic_update_slice(hidden, part[0], (0, 0, kind, r ^ mask, 0, 0))
        hidden = lax.dynamic_update_slice(hidden, part[1], (0, 0, 1 - kind, r ^ mask, 0, 0))
    return hidden.reshape(2, 1, 1, fsdp_size * group_size, capacity, half_width)


def solution(mesh):
    in_specs = (
        P("expert", None, "fsdp", None),
        P("expert", None, "fsdp", None),
        P("expert", None, "fsdp", None),
        P(None, ("fsdp", "expert"), None),
        P(None, ("fsdp", "expert"), None),
        P(),
    )
    out_specs = P(None, "fsdp", "expert", None, None, None)

    return jax.shard_map(
        on_device, mesh=mesh, in_specs=in_specs, out_specs=out_specs, check_vma=False
    )
```

```python
import functools
import math

import jax
import jax.numpy as jnp
import numpy as np
from jax import lax
from jax.experimental import pallas as pl
from jax.experimental.pallas import tpu as pltpu
from jax.sharding import PartitionSpec as P


momentum_decay = 0.95
coef_first = 3.4445
coef_second = -4.775
coef_third = 2.0315
step_size = 0.02
eps = 1e-07


VMEM = pl.BlockSpec(memory_space=pltpu.VMEM)
SMEM = pl.BlockSpec(memory_space=pltpu.SMEM)


def dot(a, b):
    return jnp.dot(a, b, preferred_element_type=jnp.float32)


def swapped(shard, axis, mask):
    return lax.ppermute(shard, axis, [(i, i ^ mask) for i in range(lax.axis_size(axis))])


def slots_of(routes, experts):
    labels = lax.broadcasted_iota(jnp.int32, (1, 1, 1, experts), 3)
    routed = jnp.any(routes[:, :, :, None] == labels, axis=2).astype(jnp.int32)
    count = routes.shape[1]
    later = lax.broadcasted_iota(jnp.int32, (count, count), 0)
    earlier = lax.broadcasted_iota(jnp.int32, (count, count), 1)
    upto = (earlier <= later).astype(jnp.int32)
    place = jnp.sum(upto[None, :, :, None] * routed[:, None, :, :], axis=2)
    return jnp.where(routed == 1, place, 0)


def gathered(block):
    fsdp_size, group_size = lax.axis_size("fsdp"), lax.axis_size("expert")
    f, r = lax.axis_index("fsdp"), lax.axis_index("expert")
    held, masks = block[None], [0]
    if group_size == 8:
        mask = 2
        while mask < fsdp_size:
            held = jnp.concatenate([held, swapped(held, "fsdp", mask)])
            masks += [m ^ mask for m in masks]
            mask *= 2
        beside = swapped(held, "expert", 2)
        opposite = swapped(held, "expert", 6)
        across = [swapped(held, "expert", 1), swapped(beside, "expert", 1)]
        last = swapped(opposite, "expert", 2)
        across += [swapped(opposite, "expert", 1), swapped(last, "expert", 1)]
        rows = jnp.concatenate([held, beside, opposite, last, *across])
        source_r = jnp.repeat(r ^ np.array([0, 2, 6, 4, 1, 3, 7, 5], np.int32), len(masks))
        source_f = jnp.tile(f ^ np.array(masks, np.int32), 8)
        return rows, source_f // 2, source_r
    held = lax.all_gather(block, "expert")
    mask = 2
    while mask < fsdp_size:
        held = jnp.concatenate([held, swapped(held, "fsdp", mask)])
        masks += [m ^ mask for m in masks]
        mask *= 2
    source_f = jnp.repeat(f ^ np.array(masks, np.int32), group_size)
    source_r = jnp.tile(jnp.arange(group_size, dtype=jnp.int32), len(masks))
    return held, source_f // 2, source_r


def columns_of(index, width):
    return pl.ds(pl.multiple_of(index * width, 128), width)


def gram_of(update_refs, total):
    for rows_ref in update_refs:
        rows = rows_ref[...]
        term = lax.dot_general(
            rows, rows, (((0,), (0,)), ((), ())), preferred_element_type=jnp.float32
        )
        total = term if total is None else total + term
    return total


def gram_kernel(*refs):
    refs[-1][...] = gram_of(refs[:-1], None)


def factor_kernel(gram_ref, *refs):
    update_refs, (factor_ref, inverse_ref) = refs[:-2], refs[-2:]
    gram = gram_of(update_refs, gram_ref[...])
    diagonal = lax.broadcasted_iota(jnp.int32, gram.shape, 0) == lax.broadcasted_iota(
        jnp.int32, gram.shape, 1
    )
    inverse = 1.0 / (jnp.sqrt(jnp.sum(jnp.where(diagonal, gram, 0.0))) + eps)
    inverse_ref[0] = inverse
    gram0 = gram * inverse * inverse
    g0 = gram0.astype(jnp.bfloat16)
    p0 = (coef_second * gram0 + coef_third * dot(g0, g0)).astype(jnp.bfloat16)
    half_way = coef_first * gram0 + dot(g0, p0)
    gram1 = coef_first * half_way + dot(half_way.astype(jnp.bfloat16), p0)
    g1 = gram1.astype(jnp.bfloat16)
    p1 = (coef_second * gram1 + coef_third * dot(g1, g1)).astype(jnp.bfloat16)
    factor = coef_first * (p0.astype(jnp.float32) + p1.astype(jnp.float32)) + dot(p0, p1)
    factor_ref[...] = factor.astype(jnp.bfloat16)


def rows_at(at_ref, place, rows_ref, depth):
    return rows_ref[:, columns_of(at_ref[0] ^ place, depth)]


def rows_from(at_ref, place, first, rows_ref, block, depth):
    start = pl.multiple_of((at_ref[0] ^ place) * block + first, 128)
    return rows_ref[:, pl.ds(start, depth)]


def along_kernel(order, sooner, scale, at_ref, inverse_ref, factor_ref, own_ref, other_ref, *refs):
    count = len(order)
    update_refs, weight_refs, (base_ref, sent_ref) = refs[:count], refs[count:-2], refs[-2:]
    width = sent_ref.shape[2]
    depth = update_refs[0].shape[0]
    own_kind = lax.rem(at_ref[0], 2)
    for side, rows_ref in enumerate((own_ref, other_ref)):
        total = sum(
            dot(rows_at(at_ref, place, rows_ref, depth), u[...])
            for place, u in zip(order, update_refs)
        )
        along = total * inverse_ref[0]
        moved = coef_first * coef_first * along + dot(along.astype(jnp.bfloat16), factor_ref[...])
        left, right = moved[:, :width], moved[:, width:]
        sent_ref[1 - side] = jnp.where(own_kind == 0, right, left).astype(jnp.bfloat16)
        kept = scale * jnp.where(own_kind == 0, left, right)
        for kind in range(2):
            product = sum(
                dot(rows_from(at_ref, *place, rows_ref, depth, weight.shape[1]), weight[kind])
                for place, weight in zip(sooner, weight_refs)
            )
            base_ref[kind, side] = product - jnp.where(own_kind == kind, kept, 0.0)


def most_kernel(place, scale, at_ref, own_ref, other_ref, base_ref, moved_ref, weight_ref, total_ref, rows_ref):
    own_kind = lax.rem(at_ref[0], 2)
    depth, last = weight_ref.shape[1], rows_ref.shape[2]
    for side, listed_ref in enumerate((own_ref, other_ref)):
        rows_ref[side] = rows_from(at_ref, place, depth, listed_ref, depth + last, last)
        rows = rows_from(at_ref, place, 0, listed_ref, depth + last, depth)
        moved = scale * moved_ref[side].astype(jnp.float32)
        for kind in range(2):
            total = base_ref[kind, side] - jnp.where(own_kind == kind, 0.0, moved)
            total_ref[kind, side] = total + dot(rows, weight_ref[kind])


def finish_kernel(at_ref, rows_ref, total_ref, weight_ref, *refs):
    out_refs, hidden = refs[:-1], refs[-1]
    for side in range(2):
        gate, up = (
            total_ref[kind, side] + dot(rows_ref[side], weight_ref[kind]) for kind in range(2)
        )
        hidden[side] = (gate / (1.0 + jnp.exp(-gate)) * up).astype(jnp.bfloat16)
    chunk = hidden.shape[1] // len(out_refs)
    for mask, out_ref in enumerate(out_refs):
        start = pl.multiple_of((at_ref[1] ^ mask) * chunk, chunk)
        out_ref[...] = hidden[:, pl.ds(start, chunk), :]


def choose_kernel(at_ref, owners_ref, *refs):
    held = refs[-1]
    count = held.shape[0]
    for mask in range(count):
        held[mask] = refs[mask][...]
    for mask in range(count):
        owner = owners_ref[at_ref[0], at_ref[1] ^ mask]
        refs[count + mask][...] = held[owner ^ at_ref[1]]


def on_device(momentum, gradient, weights, tokens, routes, owners):
    fsdp_size = lax.axis_size("fsdp")
    group_size = lax.axis_size("expert")
    per_group = fsdp_size // 2
    experts = per_group * group_size
    local_rows = momentum.shape[2]
    hidden_width = momentum.shape[3]
    half_width = hidden_width // 2
    model_width = tokens.shape[2]
    tok_dev = tokens.shape[1]
    top_count = routes.shape[2]
    capacity = max(2, 2 * tok_dev * top_count // experts)
    f = lax.axis_index("fsdp")
    r = lax.axis_index("expert")
    own_expert = r * per_group + f // 2
    at = jnp.stack([f, r]).astype(jnp.int32)
    near = [0, 1]
    far = list(range(2, fsdp_size))
    order = near + far
    weight = weights.reshape(fsdp_size, local_rows, hidden_width)

    def weight_part(weight, mask, first=0, depth=local_rows):
        target = f ^ mask
        return lax.dynamic_slice(
            weight,
            (target // 2 * 2, first, target % 2 * half_width),
            (2, depth, half_width),
        )

    lead, lead_rows = far[-1], max(128, local_rows // 4)
    early_part = weight_part(weight, lead, 0, lead_rows)
    early_part = swapped(early_part, "fsdp", lead)

    slot_lanes = -(-experts // 128) * 128
    slots = slots_of(routes, experts).astype(jnp.bfloat16)
    slots = jnp.pad(slots, ((0, 0), (0, 0), (0, slot_lanes - experts)))
    block = jnp.concatenate([tokens, slots], axis=2)
    block = block.reshape(2 * tok_dev, model_width + slot_lanes)
    block, weight = lax.optimization_barrier((block, weight))
    blocks, source_pair, source_group = gathered(block)
    all_rows = blocks.reshape(-1, model_width + slot_lanes)
    lane = lax.broadcasted_iota(jnp.int32, (1, slot_lanes), 1)
    picked = jnp.where(lane == own_expert, all_rows[:, model_width:].astype(jnp.float32), 0.0)
    slot = jnp.sum(picked, axis=1).astype(jnp.int32).reshape(-1, 2, tok_dev)
    batch = jnp.arange(2, dtype=jnp.int32)[None, :, None]
    first = (source_group[:, None, None] * 2 + batch) * per_group + source_pair[:, None, None]
    listed_at = jnp.where(slot > 0, first * capacity + slot - 1, -1).reshape(1, -1)
    half_rows = group_size * 2 * per_group * capacity
    labels = lax.broadcasted_iota(jnp.int32, (half_rows, listed_at.shape[1]), 0)
    select = (labels == listed_at).astype(jnp.bfloat16)
    own_rows = dot(select, all_rows[:, :model_width]).astype(jnp.bfloat16)
    other_rows = swapped(own_rows, "fsdp", 1)

    moment = momentum.reshape(fsdp_size, local_rows, hidden_width)
    grad = gradient.reshape(fsdp_size, local_rows, hidden_width)
    update, held_weight = [None] * fsdp_size, [None] * fsdp_size
    for places in (far, near):
        for mask in reversed(places):
            moment_part = lax.dynamic_index_in_dim(moment, f ^ mask, 0, keepdims=False)
            grad_part = lax.dynamic_index_in_dim(grad, f ^ mask, 0, keepdims=False)
            grad_part = grad_part.astype(jnp.float32)
            accumulated = momentum_decay * moment_part.astype(jnp.float32) + grad_part
            update[mask] = (grad_part + momentum_decay * accumulated).astype(jnp.bfloat16)
        if places is far:
            moment, grad, *parts = lax.optimization_barrier(
                (moment, grad, *[update[m] for m in far])
            )
            for mask, part in zip(far, parts):
                update[mask] = part
    for mask in reversed(range(1, fsdp_size)):
        update[mask] = swapped(update[mask], "fsdp", mask)
    latest, body_rows = far[0], local_rows - lead_rows
    held_weight[0] = weight_part(weight, 0)
    for mask in reversed(range(1, fsdp_size)):
        first = lead_rows if mask == lead else 0
        depth = body_rows if mask in (lead, latest) else local_rows
        part = weight_part(weight, mask, first, depth)
        held_weight[mask] = swapped(part, "fsdp", mask)
    part = weight_part(weight, latest, body_rows, lead_rows)
    last_part = swapped(part, "fsdp", latest)
    sooner = [((place, 0), held_weight[place]) for place in near + far[1:-1]]
    sooner += [((lead, 0), early_part), ((lead, lead_rows), held_weight[lead])]
    places, parts = zip(*sooner)

    full_rows = fsdp_size * local_rows
    update_scale = step_size * 0.2 * math.sqrt(max(full_rows, hidden_width))
    depth = local_rows
    bf16_scratch = lambda *shape: pltpu.VMEM(shape, jnp.bfloat16)
    shaped = lambda kind, *shape: jax.ShapeDtypeStruct(shape, kind)
    flops = 2 * 2 * half_rows * full_rows * hidden_width
    cost = lambda work, moved_bytes: pl.CostEstimate(
        flops=work, bytes_accessed=moved_bytes, transcendentals=0
    )
    limit = lambda mebibytes: pltpu.CompilerParams(vmem_limit_bytes=mebibytes << 20)
    early, late = near + far[1:], far[:1]
    gram = pl.pallas_call(
        gram_kernel,
        out_shape=shaped(jnp.float32, hidden_width, hidden_width),
        in_specs=[VMEM] * len(early),
        out_specs=VMEM,
        compiler_params=limit(8),
        cost_estimate=cost(flops, 4 << 20),
        name="gram",
    )(*[update[m] for m in early])
    factor, inverse = pl.pallas_call(
        factor_kernel,
        out_shape=[
            shaped(jnp.bfloat16, hidden_width, hidden_width),
            shaped(jnp.float32, 1),
        ],
        in_specs=[VMEM] * (1 + len(late)),
        out_specs=[VMEM, SMEM],
        compiler_params=limit(14),
        cost_estimate=cost(2 * flops, 4 << 20),
        name="factor",
    )(gram, *[update[m] for m in late])

    kind = f % 2
    half_shape = (2, half_rows, half_width)
    base, sent = pl.pallas_call(
        functools.partial(along_kernel, order, places, update_scale),
        out_shape=[
            shaped(jnp.float32, 2, *half_shape),
            shaped(jnp.bfloat16, *half_shape),
        ],
        in_specs=[SMEM, SMEM] + [VMEM] * (3 + len(order) + len(sooner)),
        out_specs=[VMEM, VMEM],
        cost_estimate=cost(2 * flops, 12 << 20),
        compiler_params=limit(10),
        name="along",
    )(
        at,
        inverse,
        factor,
        own_rows,
        other_rows,
        *[update[m] for m in order],
        *parts,
    )
    partner = swapped(sent, "fsdp", 1)
    chunk = half_rows // group_size
    total, rows_left = pl.pallas_call(
        functools.partial(most_kernel, latest, update_scale),
        out_shape=[
            shaped(jnp.float32, 2, *half_shape),
            shaped(jnp.bfloat16, 2, half_rows, lead_rows),
        ],
        in_specs=[SMEM] + [VMEM] * 5,
        out_specs=[VMEM, VMEM],
        cost_estimate=cost(flops // 4, 8 << 20),
        compiler_params=limit(8),
        name="most",
    )(at, own_rows, other_rows, base, partner, held_weight[latest])
    pieces = pl.pallas_call(
        finish_kernel,
        out_shape=[shaped(jnp.bfloat16, 2, chunk, half_width)] * group_size,
        in_specs=[SMEM] + [VMEM] * 3,
        out_specs=[VMEM] * group_size,
        scratch_shapes=[bf16_scratch(*half_shape)],
        cost_estimate=cost(flops // 8, 4 << 20),
        compiler_params=limit(8),
        name="finish",
    )(at, rows_left, total, last_part)

    spread = [swapped(pieces[m], "expert", m) if m else pieces[m] for m in range(group_size)]
    part_shape = spread[0].shape
    chosen = pl.pallas_call(
        choose_kernel,
        out_shape=[shaped(jnp.bfloat16, *part_shape)] * group_size,
        in_specs=[SMEM, SMEM] + [VMEM] * group_size,
        out_specs=[VMEM] * group_size,
        scratch_shapes=[bf16_scratch(group_size, *part_shape)],
        cost_estimate=cost(0, 2 << 20),
        compiler_params=limit(8),
        name="choose",
    )(at, owners, *spread)
    hidden = jnp.zeros((2, per_group, 2, group_size, capacity, half_width), jnp.bfloat16)
    for mask in range(group_size):
        part = chosen[mask]
        part = swapped(part, "expert", mask) if mask else part
        part = part.reshape(2, 2, per_group, 1, 1, capacity, half_width)
        hidden = lax.dynamic_update_slice(hidden, part[0], (0, 0, kind, r ^ mask, 0, 0))
        hidden = lax.dynamic_update_slice(hidden, part[1], (0, 0, 1 - kind, r ^ mask, 0, 0))
    return hidden.reshape(2, 1, 1, fsdp_size * group_size, capacity, half_width)


def solution(mesh):
    in_specs = (
        P("expert", None, "fsdp", None),
        P("expert", None, "fsdp", None),
        P("expert", None, "fsdp", None),
        P(None, ("fsdp", "expert"), None),
        P(None, ("fsdp", "expert"), None),
        P(),
    )
    out_specs = P(None, "fsdp", "expert", None, None, None)

    return jax.shard_map(
        on_device, mesh=mesh, in_specs=in_specs, out_specs=out_specs, check_vma=False
    )
```

```python
import functools
import math

import jax
import jax.numpy as jnp
import numpy as np
from jax import lax
from jax.experimental import pallas as pl
from jax.experimental.pallas import tpu as pltpu
from jax.sharding import PartitionSpec as P


momentum_decay = 0.95
coef_first = 3.4445
coef_second = -4.775
coef_third = 2.0315
step_size = 0.02
eps = 1e-07


VMEM = pl.BlockSpec(memory_space=pltpu.VMEM)
SMEM = pl.BlockSpec(memory_space=pltpu.SMEM)


def dot(a, b):
    return jnp.dot(a, b, preferred_element_type=jnp.float32)


def swapped(shard, axis, mask):
    return lax.ppermute(shard, axis, [(i, i ^ mask) for i in range(lax.axis_size(axis))])


def slots_of(routes, experts):
    labels = lax.broadcasted_iota(jnp.int32, (1, 1, 1, experts), 3)
    routed = jnp.any(routes[:, :, :, None] == labels, axis=2).astype(jnp.int32)
    count = routes.shape[1]
    later = lax.broadcasted_iota(jnp.int32, (count, count), 0)
    earlier = lax.broadcasted_iota(jnp.int32, (count, count), 1)
    upto = (earlier <= later).astype(jnp.int32)
    place = jnp.sum(upto[None, :, :, None] * routed[:, None, :, :], axis=2)
    return jnp.where(routed == 1, place, 0)


def gathered(tokens, slots, sent):
    fsdp_size, group_size = lax.axis_size("fsdp"), lax.axis_size("expert")
    f, r = lax.axis_index("fsdp"), lax.axis_index("expert")
    block = jnp.concatenate([tokens, slots], axis=1)
    held, masks = block[None], [0]
    if group_size == 8:
        mask = 2
        came = jnp.concatenate([sent, swapped(slots, "fsdp", mask)], axis=1)
        held, masks = jnp.stack([block, came]), [0, mask]
        mask = 4
        while mask < fsdp_size:
            held = jnp.concatenate([held, swapped(held, "fsdp", mask)])
            masks += [m ^ mask for m in masks]
            mask *= 2
        beside = swapped(held, "expert", 2)
        opposite = swapped(held, "expert", 6)
        across = [swapped(held, "expert", 1), swapped(beside, "expert", 1)]
        last = swapped(opposite, "expert", 2)
        across += [swapped(opposite, "expert", 1), swapped(last, "expert", 1)]
        rows = jnp.concatenate([held, beside, opposite, last, *across])
        source_r = jnp.repeat(r ^ np.array([0, 2, 6, 4, 1, 3, 7, 5], np.int32), len(masks))
        source_f = jnp.tile(f ^ np.array(masks, np.int32), 8)
        return rows, source_f // 2, source_r
    held = lax.all_gather(block, "expert")
    mask = 2
    while mask < fsdp_size:
        held = jnp.concatenate([held, swapped(held, "fsdp", mask)])
        masks += [m ^ mask for m in masks]
        mask *= 2
    source_f = jnp.repeat(f ^ np.array(masks, np.int32), group_size)
    source_r = jnp.tile(jnp.arange(group_size, dtype=jnp.int32), len(masks))
    return held, source_f // 2, source_r


def columns_of(index, width):
    return pl.ds(pl.multiple_of(index * width, 128), width)


def gram_of(update_refs, total):
    for rows_ref in update_refs:
        rows = rows_ref[...]
        term = lax.dot_general(
            rows, rows, (((0,), (0,)), ((), ())), preferred_element_type=jnp.float32
        )
        total = term if total is None else total + term
    return total


def gram_kernel(*refs):
    refs[-1][...] = gram_of(refs[:-1], None)


def factor_kernel(gram_ref, *refs):
    update_refs, (factor_ref, inverse_ref) = refs[:-2], refs[-2:]
    gram = gram_of(update_refs, gram_ref[...])
    diagonal = lax.broadcasted_iota(jnp.int32, gram.shape, 0) == lax.broadcasted_iota(
        jnp.int32, gram.shape, 1
    )
    inverse = 1.0 / (jnp.sqrt(jnp.sum(jnp.where(diagonal, gram, 0.0))) + eps)
    inverse_ref[0] = inverse
    gram0 = gram * inverse * inverse
    g0 = gram0.astype(jnp.bfloat16)
    p0 = (coef_second * gram0 + coef_third * dot(g0, g0)).astype(jnp.bfloat16)
    half_way = coef_first * gram0 + dot(g0, p0)
    gram1 = coef_first * half_way + dot(half_way.astype(jnp.bfloat16), p0)
    g1 = gram1.astype(jnp.bfloat16)
    p1 = (coef_second * gram1 + coef_third * dot(g1, g1)).astype(jnp.bfloat16)
    factor = coef_first * (p0.astype(jnp.float32) + p1.astype(jnp.float32)) + dot(p0, p1)
    factor_ref[...] = factor.astype(jnp.bfloat16)


def rows_at(at_ref, place, rows_ref, depth):
    return rows_ref[:, columns_of(at_ref[0] ^ place, depth)]


def rows_from(at_ref, place, first, rows_ref, block, depth):
    start = pl.multiple_of((at_ref[0] ^ place) * block + first, 128)
    return rows_ref[:, pl.ds(start, depth)]


def along_kernel(order, sooner, scale, at_ref, inverse_ref, factor_ref, own_ref, other_ref, *refs):
    count = len(order)
    update_refs, weight_refs, (base_ref, sent_ref) = refs[:count], refs[count:-2], refs[-2:]
    width = sent_ref.shape[2]
    depth = update_refs[0].shape[0]
    own_kind = lax.rem(at_ref[0], 2)
    for side, rows_ref in enumerate((own_ref, other_ref)):
        total = sum(
            dot(rows_at(at_ref, place, rows_ref, depth), u[...])
            for place, u in zip(order, update_refs)
        )
        along = total * inverse_ref[0]
        moved = coef_first * coef_first * along + dot(along.astype(jnp.bfloat16), factor_ref[...])
        left, right = moved[:, :width], moved[:, width:]
        sent_ref[1 - side] = jnp.where(own_kind == 0, right, left).astype(jnp.bfloat16)
        kept = scale * jnp.where(own_kind == 0, left, right)
        for kind in range(2):
            product = sum(
                dot(rows_from(at_ref, *place, rows_ref, depth, weight.shape[1]), weight[kind])
                for place, weight in zip(sooner, weight_refs)
            )
            base_ref[kind, side] = product - jnp.where(own_kind == kind, kept, 0.0)


def most_kernel(place, scale, at_ref, own_ref, other_ref, base_ref, moved_ref, weight_ref, total_ref, rows_ref):
    own_kind = lax.rem(at_ref[0], 2)
    depth, last = weight_ref.shape[1], rows_ref.shape[2]
    for side, listed_ref in enumerate((own_ref, other_ref)):
        rows_ref[side] = rows_from(at_ref, place, depth, listed_ref, depth + last, last)
        rows = rows_from(at_ref, place, 0, listed_ref, depth + last, depth)
        moved = scale * moved_ref[side].astype(jnp.float32)
        for kind in range(2):
            total = base_ref[kind, side] - jnp.where(own_kind == kind, 0.0, moved)
            total_ref[kind, side] = total + dot(rows, weight_ref[kind])


def finish_kernel(at_ref, rows_ref, total_ref, weight_ref, *refs):
    out_refs, hidden = refs[:-1], refs[-1]
    for side in range(2):
        gate, up = (
            total_ref[kind, side] + dot(rows_ref[side], weight_ref[kind]) for kind in range(2)
        )
        hidden[side] = (gate / (1.0 + jnp.exp(-gate)) * up).astype(jnp.bfloat16)
    chunk = hidden.shape[1] // len(out_refs)
    for mask, out_ref in enumerate(out_refs):
        start = pl.multiple_of((at_ref[1] ^ mask) * chunk, chunk)
        out_ref[...] = hidden[:, pl.ds(start, chunk), :]


def choose_kernel(at_ref, owners_ref, *refs):
    held = refs[-1]
    count = held.shape[0]
    for mask in range(count):
        held[mask] = refs[mask][...]
    for mask in range(count):
        owner = owners_ref[at_ref[0], at_ref[1] ^ mask]
        refs[count + mask][...] = held[owner ^ at_ref[1]]


def on_device(momentum, gradient, weights, tokens, routes, owners):
    fsdp_size = lax.axis_size("fsdp")
    group_size = lax.axis_size("expert")
    per_group = fsdp_size // 2
    experts = per_group * group_size
    local_rows = momentum.shape[2]
    hidden_width = momentum.shape[3]
    half_width = hidden_width // 2
    model_width = tokens.shape[2]
    tok_dev = tokens.shape[1]
    top_count = routes.shape[2]
    capacity = max(2, 2 * tok_dev * top_count // experts)
    f = lax.axis_index("fsdp")
    r = lax.axis_index("expert")
    own_expert = r * per_group + f // 2
    at = jnp.stack([f, r]).astype(jnp.int32)
    near = [0, 1]
    far = list(range(2, fsdp_size))
    order = near + far
    weight = weights.reshape(fsdp_size, local_rows, hidden_width)

    def weight_part(weight, mask, first=0, depth=local_rows):
        target = f ^ mask
        return lax.dynamic_slice(
            weight,
            (target // 2 * 2, first, target % 2 * half_width),
            (2, depth, half_width),
        )

    token_rows = tokens.reshape(2 * tok_dev, model_width)
    token_sent = swapped(token_rows, "fsdp", 2)
    lead, lead_rows = far[-1], max(128, local_rows // 4)
    early_part = weight_part(weight, lead, 0, lead_rows)
    early_part = swapped(early_part, "fsdp", lead)

    slot_lanes = -(-experts // 128) * 128
    slots = slots_of(routes, experts).astype(jnp.bfloat16)
    slots = jnp.pad(slots, ((0, 0), (0, 0), (0, slot_lanes - experts)))
    slots = slots.reshape(2 * tok_dev, slot_lanes)
    blocks, source_pair, source_group = gathered(token_rows, slots, token_sent)
    all_rows = blocks.reshape(-1, model_width + slot_lanes)
    lane = lax.broadcasted_iota(jnp.int32, (1, slot_lanes), 1)
    picked = jnp.where(lane == own_expert, all_rows[:, model_width:].astype(jnp.float32), 0.0)
    slot = jnp.sum(picked, axis=1).astype(jnp.int32).reshape(-1, 2, tok_dev)
    batch = jnp.arange(2, dtype=jnp.int32)[None, :, None]
    first = (source_group[:, None, None] * 2 + batch) * per_group + source_pair[:, None, None]
    listed_at = jnp.where(slot > 0, first * capacity + slot - 1, -1).reshape(1, -1)
    half_rows = group_size * 2 * per_group * capacity
    labels = lax.broadcasted_iota(jnp.int32, (half_rows, listed_at.shape[1]), 0)
    select = (labels == listed_at).astype(jnp.bfloat16)
    own_rows = dot(select, all_rows[:, :model_width]).astype(jnp.bfloat16)
    other_rows = swapped(own_rows, "fsdp", 1)

    moment = momentum.reshape(fsdp_size, local_rows, hidden_width)
    grad = gradient.reshape(fsdp_size, local_rows, hidden_width)
    update, held_weight = [None] * fsdp_size, [None] * fsdp_size
    for places in (far, near):
        for mask in reversed(places):
            moment_part = lax.dynamic_index_in_dim(moment, f ^ mask, 0, keepdims=False)
            grad_part = lax.dynamic_index_in_dim(grad, f ^ mask, 0, keepdims=False)
            grad_part = grad_part.astype(jnp.float32)
            accumulated = momentum_decay * moment_part.astype(jnp.float32) + grad_part
            update[mask] = (grad_part + momentum_decay * accumulated).astype(jnp.bfloat16)
        if places is far:
            moment, grad, *parts = lax.optimization_barrier(
                (moment, grad, *[update[m] for m in far])
            )
            for mask, part in zip(far, parts):
                update[mask] = part
    for mask in reversed(range(1, fsdp_size)):
        update[mask] = swapped(update[mask], "fsdp", mask)
    latest, body_rows = far[0], local_rows - lead_rows
    held_weight[0] = weight_part(weight, 0)
    for mask in reversed(range(1, fsdp_size)):
        first = lead_rows if mask == lead else 0
        depth = body_rows if mask in (lead, latest) else local_rows
        part = weight_part(weight, mask, first, depth)
        held_weight[mask] = swapped(part, "fsdp", mask)
    part = weight_part(weight, latest, body_rows, lead_rows)
    last_part = swapped(part, "fsdp", latest)
    sooner = [((place, 0), held_weight[place]) for place in near + far[1:-1]]
    sooner += [((lead, 0), early_part), ((lead, lead_rows), held_weight[lead])]
    places, parts = zip(*sooner)

    full_rows = fsdp_size * local_rows
    update_scale = step_size * 0.2 * math.sqrt(max(full_rows, hidden_width))
    depth = local_rows
    bf16_scratch = lambda *shape: pltpu.VMEM(shape, jnp.bfloat16)
    shaped = lambda kind, *shape: jax.ShapeDtypeStruct(shape, kind)
    flops = 2 * 2 * half_rows * full_rows * hidden_width
    cost = lambda work, moved_bytes: pl.CostEstimate(
        flops=work, bytes_accessed=moved_bytes, transcendentals=0
    )
    limit = lambda mebibytes: pltpu.CompilerParams(vmem_limit_bytes=mebibytes << 20)
    early, late = near + far[1:], far[:1]
    gram = pl.pallas_call(
        gram_kernel,
        out_shape=shaped(jnp.float32, hidden_width, hidden_width),
        in_specs=[VMEM] * len(early),
        out_specs=VMEM,
        compiler_params=limit(8),
        cost_estimate=cost(flops, 4 << 20),
        name="gram",
    )(*[update[m] for m in early])
    factor, inverse = pl.pallas_call(
        factor_kernel,
        out_shape=[
            shaped(jnp.bfloat16, hidden_width, hidden_width),
            shaped(jnp.float32, 1),
        ],
        in_specs=[VMEM] * (1 + len(late)),
        out_specs=[VMEM, SMEM],
        compiler_params=limit(14),
        cost_estimate=cost(2 * flops, 4 << 20),
        name="factor",
    )(gram, *[update[m] for m in late])

    kind = f % 2
    half_shape = (2, half_rows, half_width)
    base, sent = pl.pallas_call(
        functools.partial(along_kernel, order, places, update_scale),
        out_shape=[
            shaped(jnp.float32, 2, *half_shape),
            shaped(jnp.bfloat16, *half_shape),
        ],
        in_specs=[SMEM, SMEM] + [VMEM] * (3 + len(order) + len(sooner)),
        out_specs=[VMEM, VMEM],
        cost_estimate=cost(2 * flops, 12 << 20),
        compiler_params=limit(10),
        name="along",
    )(
        at,
        inverse,
        factor,
        own_rows,
        other_rows,
        *[update[m] for m in order],
        *parts,
    )
    partner = swapped(sent, "fsdp", 1)
    chunk = half_rows // group_size
    total, rows_left = pl.pallas_call(
        functools.partial(most_kernel, latest, update_scale),
        out_shape=[
            shaped(jnp.float32, 2, *half_shape),
            shaped(jnp.bfloat16, 2, half_rows, lead_rows),
        ],
        in_specs=[SMEM] + [VMEM] * 5,
        out_specs=[VMEM, VMEM],
        cost_estimate=cost(flops // 4, 8 << 20),
        compiler_params=limit(8),
        name="most",
    )(at, own_rows, other_rows, base, partner, held_weight[latest])
    pieces = pl.pallas_call(
        finish_kernel,
        out_shape=[shaped(jnp.bfloat16, 2, chunk, half_width)] * group_size,
        in_specs=[SMEM] + [VMEM] * 3,
        out_specs=[VMEM] * group_size,
        scratch_shapes=[bf16_scratch(*half_shape)],
        cost_estimate=cost(flops // 8, 4 << 20),
        compiler_params=limit(8),
        name="finish",
    )(at, rows_left, total, last_part)

    spread = [swapped(pieces[m], "expert", m) if m else pieces[m] for m in range(group_size)]
    part_shape = spread[0].shape
    chosen = pl.pallas_call(
        choose_kernel,
        out_shape=[shaped(jnp.bfloat16, *part_shape)] * group_size,
        in_specs=[SMEM, SMEM] + [VMEM] * group_size,
        out_specs=[VMEM] * group_size,
        scratch_shapes=[bf16_scratch(group_size, *part_shape)],
        cost_estimate=cost(0, 2 << 20),
        compiler_params=limit(8),
        name="choose",
    )(at, owners, *spread)
    hidden = jnp.zeros((2, per_group, 2, group_size, capacity, half_width), jnp.bfloat16)
    for mask in range(group_size):
        part = chosen[mask]
        part = swapped(part, "expert", mask) if mask else part
        part = part.reshape(2, 2, per_group, 1, 1, capacity, half_width)
        hidden = lax.dynamic_update_slice(hidden, part[0], (0, 0, kind, r ^ mask, 0, 0))
        hidden = lax.dynamic_update_slice(hidden, part[1], (0, 0, 1 - kind, r ^ mask, 0, 0))
    return hidden.reshape(2, 1, 1, fsdp_size * group_size, capacity, half_width)


def solution(mesh):
    in_specs = (
        P("expert", None, "fsdp", None),
        P("expert", None, "fsdp", None),
        P("expert", None, "fsdp", None),
        P(None, ("fsdp", "expert"), None),
        P(None, ("fsdp", "expert"), None),
        P(),
    )
    out_specs = P(None, "fsdp", "expert", None, None, None)

    return jax.shard_map(
        on_device, mesh=mesh, in_specs=in_specs, out_specs=out_specs, check_vma=False
    )
```
